32 devices in a mesh: row: 16 (over z, y, core), col: 2 (over x).
Axes of the slice: x: 2, y: 2, z: 4, core: 2. Of those that a mesh axis runs over, the one named last changes fastest.
Arguments:
- pair: bfloat16 [384, 384, 128], P('row', 'col'), may hold values from -6 to 6
- gain: float32 [128], replicated, may hold values from 0.1 to 1.9
- projections: bfloat16 [5, 128, 128], replicated, may hold values from -0.5 to 0.5
- bias_weight: bfloat16 [128, 4], replicated, as said below
- valid_len: int32 [1], replicated, may hold values from 192 to 384
- out_cotangent: bfloat16 [384, 384, 128], P('row', 'col'), may hold values from -6 to 6
Outputs:
- attended: bfloat16 [384, 384, 128], P('row', 'col')
- pair_gradient: float32 [384, 384, 128], P('row', 'col')
- projection_grad: float32 [5, 128, 128], replicated
- bias_weight_grad: float32 [128, 4], replicated
- gain_gradient: float32 [128], replicated
The draws below stay inside these ranges and needn't reach their ends.
Inputs may be any that keep to these rules, and one draw needn't show every extreme that they name: `bias_weight`: scale of the bias projection entries is free; rows are drawn independently.
All inputs are finite; a program needn't handle non-finite values.
Results may differ from the reference program's by a relative error of at most 0.0045.
The reference program's roundings to bfloat16 on the way count: a program that leaves them out, or rounds other values in their place, can miss the bound.
Values may be sent and summed in bfloat16 or wider, within the bound.
A program may use at most 64 MiB of HBM per device.

```python
import jax
import jax.numpy as jnp
from jax import lax

C = 128
H = 4
QB = 384
N = 384


def draw_bias_weight(key, part):
    base = jax.random.normal(jax.random.fold_in(key, 17), (C, H), jnp.float32) * C ** (-0.5)
    return base.astype(jnp.bfloat16)


def level_of(stream_key, shape, pieces, low, high):
    def one(position, shards_of):
        steps = jax.random.uniform(jax.random.fold_in(jax.random.fold_in(stream_key, 6), position), (shards_of,), jnp.float32, low / len(pieces), high / len(pieces))
        return jnp.repeat(jnp.exp(steps), shape[position] // shards_of).reshape((-1,) + (1,) * (len(shape) - position - 1))

    factor_of = one(*pieces[0])
    for cut in pieces[1:]:
        factor_of = factor_of * one(*cut)
    return factor_of


def normal_values(rng, shape, deviation, limit, pieces=(), kind=jnp.bfloat16):
    factor_of = level_of(rng, shape, pieces, -0.22, 0.18) if pieces else 1.0
    array = jax.random.normal(rng, shape, jnp.float32) * deviation * factor_of
    return jnp.minimum(jnp.maximum(array, -limit), limit).astype(kind)


def setup_inputs(seed: int = 0) -> dict:
    key_list = jax.random.split(jax.random.key(seed), 7)
    pair = normal_values(key_list[0], (N, N, C), 1.0, 6.0, ((0, 16), (1, 2)))
    gain = jnp.clip(1.0 + 0.18 * jax.random.normal(key_list[1], (C,), jnp.float32), 0.1, 1.9)
    projections = normal_values(key_list[2], (5, C, C), C ** -0.5, 0.5)
    bias_weight = draw_bias_weight(jax.random.fold_in(key_list[6], 71), 0)
    valid_len = jax.random.randint(key_list[4], (1,), N // 2, N + 1).astype(jnp.int32)
    out_cotangent = normal_values(key_list[5], (N, N, C), 1.0, 6.0, ((0, 16), (1, 2)))
    return dict(pair=pair, gain=gain, projections=projections, bias_weight=bias_weight, valid_len=valid_len, out_cotangent=out_cotangent)


EPS = 1e-05

def dense(left, right):
    return jnp.einsum('abc,cd->abd', left.astype(jnp.float32), right.astype(jnp.float32))

def outer_sum(left, right):
    return jnp.einsum('abc,abd->cd', left.astype(jnp.float32), right.astype(jnp.float32))

def attend_forward(query, key, value, bias_blocks, keep):
    ncols, rows, heads, width = query.shape
    nblocks = bias_blocks.shape[0]
    scale = width ** (-0.5)

    def per_column(cols):
        qcol, kcol, vcol = cols

        def per_block(blk):
            qblk, bblk = blk
            scores = jnp.einsum('qhd,khd->hqk', qblk.astype(jnp.float32), kcol.astype(jnp.float32)) * scale + bblk.astype(jnp.float32)
            scores = jnp.where(keep[None, None, :], scores, -1000000000.0)
            probs = jax.nn.softmax(scores, axis=-1)
            out = jnp.einsum('hqk,khd->qhd', probs.astype(jnp.bfloat16).astype(jnp.float32), vcol.astype(jnp.float32))
            return out.astype(jnp.bfloat16)
        return lax.map(per_block, (qcol.reshape(nblocks, rows // nblocks, heads, width), bias_blocks)).reshape(rows, heads, width)
    return lax.map(per_column, (query, key, value))

def attend_backward(query, key, value, d_context, bias_blocks, keep):
    ncols, rows, heads, width = query.shape
    nblocks = bias_blocks.shape[0]
    qsize = rows // nblocks
    scale = width ** (-0.5)

    def per_column(total, cols):
        qcol, kcol, vcol, dcol = cols

        def per_block(carry, blk):
            dk_acc, dv_acc = carry
            qblk, dblk, bblk = blk
            scores = jnp.einsum('qhd,khd->hqk', qblk.astype(jnp.float32), kcol.astype(jnp.float32)) * scale + bblk.astype(jnp.float32)
            scores = jnp.where(keep[None, None, :], scores, -1000000000.0)
            probs = jax.nn.softmax(scores, axis=-1)
            weights_b = probs.astype(jnp.bfloat16).astype(jnp.float32)
            d_probs = jnp.einsum('qhd,khd->hqk', dblk.astype(jnp.float32), vcol.astype(jnp.float32))
            d_scores = probs * (d_probs - lax.optimization_barrier(jnp.sum(probs * d_probs, axis=-1, keepdims=True)))
            dsb = d_scores.astype(jnp.bfloat16).astype(jnp.float32)
            dq = (jnp.einsum('hqk,khd->qhd', dsb, kcol.astype(jnp.float32)) * scale).astype(jnp.bfloat16)
            dk_acc = dk_acc + jnp.einsum('hqk,qhd->khd', dsb, qblk.astype(jnp.float32)) * scale
            dv_acc = dv_acc + jnp.einsum('hqk,qhd->khd', weights_b, dblk.astype(jnp.float32))
            return ((dk_acc, dv_acc), (dq, d_scores))
        zeros = jnp.zeros((rows, heads, width), jnp.float32)
        (dk, dv), (dq, dscores) = lax.scan(per_block, (zeros, zeros), (qcol.reshape(nblocks, qsize, heads, width), dcol.reshape(nblocks, qsize, heads, width), bias_blocks))
        return (total + dscores, (dq.reshape(rows, heads, width), dk.astype(jnp.bfloat16), dv.astype(jnp.bfloat16)))
    start = jnp.zeros(bias_blocks.shape, jnp.float32)
    total, (dq, dk, dv) = lax.scan(per_column, start, (query, key, value, d_context))
    return (dq, dk, dv, total)

def reference(pair, gain, projections, bias_weight, valid_len, out_cotangent):
    heads = bias_weight.shape[1]
    width = pair.shape[2] // heads
    rows = pair.shape[0]
    pair_float = pair.astype(jnp.float32)
    average_value = lax.optimization_barrier(jnp.mean(pair_float, axis=-1, keepdims=True))
    var = lax.optimization_barrier(jnp.mean((pair_float - average_value) ** 2, axis=-1, keepdims=True))
    inverse_deviation = lax.rsqrt(var + EPS)
    centered_scaled = (pair_float - average_value) * inverse_deviation
    normalized_pair = (centered_scaled * gain).astype(jnp.bfloat16)
    query = dense(normalized_pair, projections[0]).astype(jnp.bfloat16)
    key = dense(normalized_pair, projections[1]).astype(jnp.bfloat16)
    value = dense(normalized_pair, projections[2]).astype(jnp.bfloat16)
    gate = jax.nn.sigmoid(dense(normalized_pair, projections[3]))
    pair_bias = dense(normalized_pair, bias_weight)
    bias_t = jnp.transpose(pair_bias, (2, 1, 0))
    bias_blocks = bias_t.reshape(heads, rows // QB, QB, rows).transpose(1, 0, 2, 3)
    keep = jnp.arange(rows, dtype=jnp.int32) < valid_len[0]

    def split(tensor):
        return jnp.moveaxis(tensor, 1, 0).reshape(rows, rows, heads, width)

    def join(tensor):
        return jnp.moveaxis(tensor.reshape(rows, rows, heads * width), 0, 1)
    context = join(attend_forward(split(query), split(key), split(value), bias_blocks, keep))
    gated = (gate * context.astype(jnp.float32)).astype(jnp.bfloat16)
    attended = dense(gated, projections[4]).astype(jnp.bfloat16)
    d_gated = dense(out_cotangent, projections[4].T)
    d_context = (d_gated * gate).astype(jnp.bfloat16)
    d_gate_pre = (d_gated * context.astype(jnp.float32) * gate * (1.0 - gate)).astype(jnp.bfloat16)
    dq, dk, dv, total = attend_backward(split(query), split(key), split(value), split(d_context), bias_blocks, keep)
    dq, dk, dv = (join(dq), join(dk), join(dv))
    d_bias_t = total.transpose(1, 0, 2, 3).reshape(heads, rows, rows)
    d_bias = jnp.transpose(d_bias_t, (2, 1, 0)).astype(jnp.bfloat16)
    normalized_gradient = dense(dq, projections[0].T) + dense(dk, projections[1].T) + dense(dv, projections[2].T)
    normalized_gradient = normalized_gradient + dense(d_gate_pre, projections[3].T) + dense(d_bias, bias_weight.T)
    projection_grad = jnp.stack([outer_sum(normalized_pair, dq), outer_sum(normalized_pair, dk), outer_sum(normalized_pair, dv), outer_sum(normalized_pair, d_gate_pre), outer_sum(gated, out_cotangent)])
    bias_weight_grad = outer_sum(normalized_pair, d_bias)
    gain_gradient = lax.optimization_barrier(jnp.sum(normalized_gradient * centered_scaled, axis=(0, 1)))
    scaled_output = normalized_gradient * gain
    pair_gradient = inverse_deviation * (scaled_output - lax.optimization_barrier(jnp.mean(scaled_output, axis=-1, keepdims=True)) - centered_scaled * lax.optimization_barrier(jnp.mean(scaled_output * centered_scaled, axis=-1, keepdims=True)))
    return (attended, pair_gradient, projection_grad, bias_weight_grad, gain_gradient)
```

```python
import functools

import jax
import jax.numpy as jnp
from jax import lax
from jax.experimental import pallas as pl
from jax.experimental.pallas import tpu as pltpu
from jax.sharding import PartitionSpec as P

EPS = 1e-05
F32 = jnp.float32
BF16 = jnp.bfloat16


def mm(left, right):
    return lax.dot_general(left, right, (((1,), (0,)), ((), ())), preferred_element_type=F32)


def mm_nt(left, right):
    return lax.dot_general(left, right, (((1,), (1,)), ((), ())), preferred_element_type=F32)


def attention_kernel(
    heads, valid_ref, x_ref, cot_ref, w_in_ref, w_out_ref, bias_ref,
    att_ref, dn_ref, dbias_ref, parts_ref, bias_s, dbias_s,
):
    step = pl.program_id(0)
    n_row, _, tile_rows, channels = x_ref.shape
    n_col, tile_cols = bias_ref.shape[1], bias_ref.shape[4]
    rows = n_row * tile_rows
    width = channels // heads
    scale = width ** (-0.5)
    keep_lanes = lax.broadcasted_iota(jnp.int32, (rows, 1), 0) < valid_ref[0]

    @pl.when(step == 0)
    def _():
        for h in range(heads):
            for c in range(n_col):
                block = bias_ref[:, c, h].reshape(rows, tile_cols)
                bias_s[h, :, c * tile_cols : (c + 1) * tile_cols] = jnp.where(
                    keep_lanes, block, -1000000000.0
                )
        dbias_s[...] = jnp.zeros_like(dbias_s)
        parts_ref[...] = jnp.zeros_like(parts_ref)

    x = x_ref[:, 0].astype(F32).reshape(rows, channels).astype(BF16)
    cot = cot_ref[:, 0].astype(F32).reshape(rows, channels).astype(BF16)
    proj = mm(x, w_in_ref[...])
    query = proj[:, :channels].astype(BF16)
    key_f = jnp.where(keep_lanes, proj[:, channels : 2 * channels], 0.0)
    key = key_f.astype(BF16)
    value_f = proj[:, 2 * channels : 3 * channels]
    value = value_f.astype(BF16)
    gate = jax.nn.sigmoid(proj[:, 3 * channels :])
    d_gated = mm_nt(cot, w_out_ref[...])
    d_context_f = d_gated * gate
    d_context = d_context_f.astype(BF16)
    key_t = jnp.transpose(key_f).astype(BF16)
    value_t = jnp.transpose(value_f).astype(BF16)
    lane_head = lax.broadcasted_iota(jnp.int32, (rows, channels), 1) // width
    ctx_parts, dq_parts = [], []
    dk = jnp.zeros((rows, channels), F32)
    dv = jnp.zeros((rows, channels), F32)
    for h in range(heads):
        mine = lane_head == h
        q_h = jnp.where(mine, query, jnp.zeros_like(query))
        dc_h = jnp.where(mine, d_context, jnp.zeros_like(d_context))
        s = mm_nt(key, q_h) * scale + bias_s[h]
        e = jnp.exp(s - jnp.max(s, axis=0, keepdims=True))
        p = e * (1.0 / jnp.sum(e, axis=0, keepdims=True))
        d_p = mm_nt(value, dc_h)
        delta = jnp.sum(p * d_p, axis=0, keepdims=True)
        ds = p * (d_p - delta)
        dbias_s[h] += ds
        p_b = p.astype(BF16)
        ds_b = ds.astype(BF16)
        ctx_parts.append(mm(value_t[h * width : (h + 1) * width], p_b))
        dq_parts.append(mm(key_t[h * width : (h + 1) * width], ds_b))
        dv += mm(p_b, dc_h)
        dk += mm(ds_b, q_h)
    context = jnp.transpose(jnp.concatenate(ctx_parts, axis=0)).astype(BF16).astype(F32)
    dq = (jnp.transpose(jnp.concatenate(dq_parts, axis=0)) * scale).astype(BF16)
    dk = (dk * scale).astype(BF16)
    dv = dv.astype(BF16)
    gated_f = gate * context
    gated = gated_f.astype(BF16)
    att = mm(gated, w_out_ref[...])
    att_ref[:, 0] = att.reshape(n_row, tile_rows, channels).astype(att_ref.dtype)
    d_gate = (d_gated * context * gate * (1.0 - gate)).astype(BF16)
    grads = jnp.concatenate([dq, dk, dv, d_gate], axis=1)
    dn = mm_nt(grads, w_in_ref[...])
    dn_ref[:, 0] = dn.reshape(n_row, tile_rows, channels).astype(dn_ref.dtype)
    x_t = jnp.transpose(x.astype(F32)).astype(BF16)
    parts_ref[:, : 4 * channels] += mm(x_t, grads)
    gated_t = jnp.transpose(gated.astype(F32)).astype(BF16)
    parts_ref[:, 4 * channels :] += mm(gated_t, cot)

    @pl.when(step == pl.num_programs(0) - 1)
    def _():
        for h in range(heads):
            for c in range(n_col):
                block = dbias_s[h, :, c * tile_cols : (c + 1) * tile_cols]
                dbias_ref[:, c, h] = block.reshape(n_row, tile_rows, tile_cols)


def attention(valid_len, x_cols, cot_cols, w_in, w_out, bias):
    n_row, ncols, tile_rows, channels = x_cols.shape
    heads, n_col, tile_cols = bias.shape[2], bias.shape[1], bias.shape[4]
    rows = n_row * tile_rows
    column = pl.BlockSpec((n_row, 1, tile_rows, channels), lambda j: (0, j, 0, 0))

    def whole(shape):
        return pl.BlockSpec(shape, lambda j: (0,) * len(shape))

    return pl.pallas_call(
        functools.partial(attention_kernel, heads),
        grid=(ncols,),
        in_specs=[
            pl.BlockSpec(memory_space=pltpu.SMEM),
            column,
            column,
            whole(w_in.shape),
            whole(w_out.shape),
            whole(bias.shape),
        ],
        out_specs=[column, column, whole(bias.shape), whole((channels, 5 * channels))],
        out_shape=[
            jax.ShapeDtypeStruct(x_cols.shape, BF16),
            jax.ShapeDtypeStruct(x_cols.shape, BF16),
            jax.ShapeDtypeStruct(bias.shape, F32),
            jax.ShapeDtypeStruct((channels, 5 * channels), F32),
        ],
        scratch_shapes=[
            pltpu.VMEM((heads, rows, rows), F32),
            pltpu.VMEM((heads, rows, rows), F32),
        ],
        compiler_params=pltpu.CompilerParams(
            dimension_semantics=("arbitrary",), vmem_limit_bytes=60 * 1024 * 1024
        ),
    )(valid_len, x_cols, cot_cols, w_in, w_out, bias)


def shards(pair, gain, projections, bias_weight, valid_len, out_cotangent):
    n_row = lax.axis_size("row")
    n_col = lax.axis_size("col")
    tile_rows, tile_cols, channels = pair.shape
    heads = bias_weight.shape[1]
    ncols = tile_cols // n_row
    pair_float = pair.astype(F32)
    average_value = jnp.mean(pair_float, axis=-1, keepdims=True)
    var = jnp.mean((pair_float - average_value) ** 2, axis=-1, keepdims=True)
    inverse_deviation = lax.rsqrt(var + EPS)
    centered_scaled = (pair_float - average_value) * inverse_deviation
    normalized_pair = (centered_scaled * gain).astype(BF16)
    bias_tile = jnp.einsum("abc,ch->hab", normalized_pair, bias_weight, preferred_element_type=F32)
    gathered = lax.all_gather(bias_tile[None], ("row", "col"), axis=0, tiled=True)
    gathered = gathered.reshape(n_row, n_col, heads, tile_rows, tile_cols)

    def to_columns(tile):
        moved = jnp.swapaxes(tile, 0, 1).reshape(n_row, ncols, tile_rows, channels)
        return lax.all_to_all(moved, "row", split_axis=0, concat_axis=0, tiled=True)

    def to_tile(columns):
        moved = lax.all_to_all(columns, "row", split_axis=0, concat_axis=0, tiled=True)
        return jnp.swapaxes(moved.reshape(tile_cols, tile_rows, channels), 0, 1)

    x_cols, cot_cols = to_columns(normalized_pair), to_columns(out_cotangent)
    w_in = jnp.swapaxes(projections[:4], 0, 1).reshape(channels, 4 * channels)
    att_cols, dn_cols, total, parts = attention(
        valid_len, x_cols, cot_cols, w_in, projections[4], gathered
    )
    flat = total.reshape(n_row * n_col, heads, tile_rows, tile_cols)
    d_bias = lax.psum_scatter(flat, ("row", "col"), scatter_dimension=0, tiled=True)[0].astype(BF16)
    parts = lax.psum(parts, ("row", "col"))
    projection_grad = jnp.swapaxes(parts.reshape(channels, 5, channels), 0, 1)
    attended = to_tile(att_cols)
    bias_term = jnp.einsum("hab,ch->abc", d_bias, bias_weight, preferred_element_type=F32)
    bias_weight_part = jnp.einsum(
        "abc,hab->ch", normalized_pair, d_bias, preferred_element_type=F32
    )
    normalized_gradient = to_tile(dn_cols).astype(F32) + bias_term
    gain_partial_sum = jnp.sum(normalized_gradient * centered_scaled, axis=(0, 1))
    bias_weight_grad, gain_gradient = lax.psum((bias_weight_part, gain_partial_sum), ("row", "col"))
    scaled_output = normalized_gradient * gain
    pair_gradient = inverse_deviation * (
        scaled_output
        - jnp.mean(scaled_output, axis=-1, keepdims=True)
        - centered_scaled * jnp.mean(scaled_output * centered_scaled, axis=-1, keepdims=True)
    )
    return (attended, pair_gradient, projection_grad, bias_weight_grad, gain_gradient)


def solution(mesh):
    placed = (P("row", "col", None), P(), P(), P(), P(), P("row", "col", None))
    return jax.shard_map(
        shards,
        mesh=mesh,
        in_specs=placed,
        out_specs=(P("row", "col", None), P("row", "col", None), P(), P(), P()),
        check_vma=False,
    )
```

```python
import functools

import jax
import jax.numpy as jnp
from jax import lax
from jax.experimental import pallas as pl
from jax.experimental.pallas import tpu as pltpu
from jax.sharding import PartitionSpec as P

EPS = 1e-05
F32 = jnp.float32
BF16 = jnp.bfloat16


def mm(left, right):
    return lax.dot_general(left, right, (((1,), (0,)), ((), ())), preferred_element_type=F32)


def mm_nt(left, right):
    return lax.dot_general(left, right, (((1,), (1,)), ((), ())), preferred_element_type=F32)


def attention_kernel(
    heads, valid_ref, x_ref, cot_ref, w_in_ref, w_out_ref, bias_ref,
    att_ref, dn_ref, dbias_ref, parts_ref, bias_s, dbias_s,
):
    step = pl.program_id(0)
    n_row, _, tile_rows, channels = x_ref.shape
    n_col, tile_cols = bias_ref.shape[1], bias_ref.shape[4]
    rows = n_row * tile_rows
    width = channels // heads
    scale = width ** (-0.5)
    keep_lanes = lax.broadcasted_iota(jnp.int32, (rows, 1), 0) < valid_ref[0]

    @pl.when(step == 0)
    def _():
        for h in range(heads):
            for c in range(n_col):
                block = bias_ref[:, c, h].reshape(rows, tile_cols)
                bias_s[h, :, c * tile_cols : (c + 1) * tile_cols] = jnp.where(
                    keep_lanes, block, -1000000000.0
                )
        dbias_s[...] = jnp.zeros_like(dbias_s)
        parts_ref[...] = jnp.zeros_like(parts_ref)

    x = x_ref[:, 0].astype(F32).reshape(rows, channels).astype(BF16)
    cot = cot_ref[:, 0].astype(F32).reshape(rows, channels).astype(BF16)
    proj = mm(x, w_in_ref[...])
    query = proj[:, :channels].astype(BF16)
    key_f = jnp.where(keep_lanes, proj[:, channels : 2 * channels], 0.0)
    key = key_f.astype(BF16)
    value_f = proj[:, 2 * channels : 3 * channels]
    value = value_f.astype(BF16)
    gate = jax.nn.sigmoid(proj[:, 3 * channels :])
    d_gated = mm_nt(cot, w_out_ref[...])
    d_context_f = d_gated * gate
    d_context = d_context_f.astype(BF16)
    key_t = jnp.transpose(key_f).astype(BF16)
    value_t = jnp.transpose(value_f).astype(BF16)
    lane_head = lax.broadcasted_iota(jnp.int32, (rows, channels), 1) // width
    ctx_parts, dq_parts = [], []
    dk = jnp.zeros((rows, channels), F32)
    dv = jnp.zeros((rows, channels), F32)
    for h in range(heads):
        mine = lane_head == h
        q_h = jnp.where(mine, query, jnp.zeros_like(query))
        dc_h = jnp.where(mine, d_context, jnp.zeros_like(d_context))
        s = mm_nt(key, q_h) * scale + bias_s[h]
        e = jnp.exp(s - jnp.max(s, axis=0, keepdims=True))
        p = e * (1.0 / jnp.sum(e, axis=0, keepdims=True))
        d_p = mm_nt(value, dc_h)
        delta = jnp.sum(p * d_p, axis=0, keepdims=True)
        ds = p * (d_p - delta)
        dbias_s[h] += ds
        p_b = p.astype(BF16)
        ds_b = ds.astype(BF16)
        ctx_parts.append(mm(value_t[h * width : (h + 1) * width], p_b))
        dq_parts.append(mm(key_t[h * width : (h + 1) * width], ds_b))
        dv += mm(p_b, dc_h)
        dk += mm(ds_b, q_h)
    context = jnp.transpose(jnp.concatenate(ctx_parts, axis=0)).astype(BF16).astype(F32)
    dq = (jnp.transpose(jnp.concatenate(dq_parts, axis=0)) * scale).astype(BF16)
    dk = (dk * scale).astype(BF16)
    dv = dv.astype(BF16)
    gated_f = gate * context
    gated = gated_f.astype(BF16)
    att = mm(gated, w_out_ref[...])
    att_ref[:, 0] = att.reshape(n_row, tile_rows, channels).astype(att_ref.dtype)
    d_gate = (d_gated * context * gate * (1.0 - gate)).astype(BF16)
    grads = jnp.concatenate([dq, dk, dv, d_gate], axis=1)
    dn = mm_nt(grads, w_in_ref[...])
    dn_ref[:, 0] = dn.reshape(n_row, tile_rows, channels).astype(dn_ref.dtype)
    x_t = jnp.transpose(x.astype(F32)).astype(BF16)
    parts_ref[:, : 4 * channels] += mm(x_t, grads)
    gated_t = jnp.transpose(gated.astype(F32)).astype(BF16)
    parts_ref[:, 4 * channels :] += mm(gated_t, cot)

    @pl.when(step == pl.num_programs(0) - 1)
    def _():
        for h in range(heads):
            for c in range(n_col):
                block = dbias_s[h, :, c * tile_cols : (c + 1) * tile_cols]
                dbias_ref[:, c, h] = block.reshape(n_row, tile_rows, tile_cols).astype(dbias_ref.dtype)


def attention(valid_len, x_cols, cot_cols, w_in, w_out, bias):
    n_row, ncols, tile_rows, channels = x_cols.shape
    heads, n_col, tile_cols = bias.shape[2], bias.shape[1], bias.shape[4]
    rows = n_row * tile_rows
    column = pl.BlockSpec((n_row, 1, tile_rows, channels), lambda j: (0, j, 0, 0))

    def whole(shape):
        return pl.BlockSpec(shape, lambda j: (0,) * len(shape))

    return pl.pallas_call(
        functools.partial(attention_kernel, heads),
        grid=(ncols,),
        in_specs=[
            pl.BlockSpec(memory_space=pltpu.SMEM),
            column,
            column,
            whole(w_in.shape),
            whole(w_out.shape),
            whole(bias.shape),
        ],
        out_specs=[column, column, whole(bias.shape), whole((channels, 5 * channels))],
        out_shape=[
            jax.ShapeDtypeStruct(x_cols.shape, BF16),
            jax.ShapeDtypeStruct(x_cols.shape, BF16),
            jax.ShapeDtypeStruct(bias.shape, BF16),
            jax.ShapeDtypeStruct((channels, 5 * channels), F32),
        ],
        scratch_shapes=[
            pltpu.VMEM((heads, rows, rows), F32),
            pltpu.VMEM((heads, rows, rows), F32),
        ],
        compiler_params=pltpu.CompilerParams(
            dimension_semantics=("arbitrary",), vmem_limit_bytes=60 * 1024 * 1024
        ),
    )(valid_len, x_cols, cot_cols, w_in, w_out, bias)


def shards(pair, gain, projections, bias_weight, valid_len, out_cotangent):
    n_row = lax.axis_size("row")
    n_col = lax.axis_size("col")
    tile_rows, tile_cols, channels = pair.shape
    heads = bias_weight.shape[1]
    ncols = tile_cols // n_row
    pair_float = pair.astype(F32)
    average_value = jnp.mean(pair_float, axis=-1, keepdims=True)
    var = jnp.mean((pair_float - average_value) ** 2, axis=-1, keepdims=True)
    inverse_deviation = lax.rsqrt(var + EPS)
    centered_scaled = (pair_float - average_value) * inverse_deviation
    normalized_pair = (centered_scaled * gain).astype(BF16)
    bias_tile = jnp.einsum("abc,ch->hab", normalized_pair, bias_weight, preferred_element_type=F32)
    gathered = lax.all_gather(bias_tile[None], ("row", "col"), axis=0, tiled=True)
    gathered = gathered.reshape(n_row, n_col, heads, tile_rows, tile_cols)

    def to_columns(tile):
        moved = jnp.swapaxes(tile, 0, 1).reshape(n_row, ncols, tile_rows, channels)
        return lax.all_to_all(moved, "row", split_axis=0, concat_axis=0, tiled=True)

    def to_tile(columns):
        moved = lax.all_to_all(columns, "row", split_axis=0, concat_axis=0, tiled=True)
        return jnp.swapaxes(moved.reshape(tile_cols, tile_rows, channels), 0, 1)

    x_cols, cot_cols = to_columns(normalized_pair), to_columns(out_cotangent)
    w_in = jnp.swapaxes(projections[:4], 0, 1).reshape(channels, 4 * channels)
    att_cols, dn_cols, total, parts = attention(
        valid_len, x_cols, cot_cols, w_in, projections[4], gathered
    )
    everyone = ("row", "col")
    n_all = n_row * n_col

    def swap(blocks):
        return lax.all_to_all(blocks, everyone, split_axis=0, concat_axis=0, tiled=True)

    shares = swap(total.reshape(n_all, heads, tile_rows, tile_cols))
    d_bias = jnp.sum(shares.astype(F32), axis=0).astype(BF16)
    parts = jnp.swapaxes(parts.reshape(channels, 5, channels), 0, 1)
    slab = 5 * channels // n_all
    owned = jnp.sum(swap(parts.reshape(n_all, slab, channels)), axis=0)
    attended = to_tile(att_cols)
    bias_term = jnp.einsum("hab,ch->abc", d_bias, bias_weight, preferred_element_type=F32)
    bias_weight_part = jnp.einsum(
        "hab,abc->hc", d_bias, normalized_pair, preferred_element_type=F32
    )
    normalized_gradient = to_tile(dn_cols).astype(F32) + bias_term
    gain_partial_sum = jnp.sum(normalized_gradient * centered_scaled, axis=(0, 1))
    mine = jnp.concatenate([owned, bias_weight_part, gain_partial_sum[None]], axis=0)
    spread = swap(jnp.broadcast_to(mine[None], (n_all,) + mine.shape))
    projection_grad = spread[:, :slab].reshape(5, channels, channels)
    small = jnp.sum(spread[:, slab:], axis=0)
    bias_weight_grad, gain_gradient = small[:heads].T, small[heads]
    scaled_output = normalized_gradient * gain
    pair_gradient = inverse_deviation * (
        scaled_output
        - jnp.mean(scaled_output, axis=-1, keepdims=True)
        - centered_scaled * jnp.mean(scaled_output * centered_scaled, axis=-1, keepdims=True)
    )
    return (attended, pair_gradient, projection_grad, bias_weight_grad, gain_gradient)


def solution(mesh):
    placed = (P("row", "col", None), P(), P(), P(), P(), P("row", "col", None))
    return jax.shard_map(
        shards,
        mesh=mesh,
        in_specs=placed,
        out_specs=(P("row", "col", None), P("row", "col", None), P(), P(), P()),
        check_vma=False,
    )
```
